32 devices in a mesh: row: 4 (over x, core), col: 8 (over z, y).
Axes of the slice: x: 2, y: 2, z: 4, core: 2. Of those that a mesh axis runs over, the one named last changes fastest.
Arguments:
- embeddings: bfloat16 [24576, 1024], P(('row', 'col')), may hold values from -40 to 40
- doc_ids: int32 [24576], P(('row', 'col')), may hold values from 0 to 24575, each once
- valid_counts: int32 [32], P(('row', 'col')), may hold values from 384 to 768
Outputs:
- nearest: float32 [24576], P(('row', 'col'))
The draws below stay inside these ranges and needn't reach their ends.
Inputs may be any that keep to these rules, and one draw needn't show every extreme that they name: `doc_ids`: the ids are distinct.
All inputs are finite; a program needn't handle non-finite values.
Results may differ from the reference program's by a relative error of at most 0.0005.
Values may be sent and summed in bfloat16 or wider, within the bound.
No kernel may reach another device: no remote copies, remote signals or barrier semaphores. Data moves between devices by JAX's collectives and lax.ppermute only.
A program may use at most 64 MiB of HBM per device.

```python
import jax
import jax.numpy as jnp
from jax import lax

D = 1024
ROWS = 768
BAND = 4
BLOCKS = 32
DOCS = 24576


def draw_embeddings(key, part):
    base_key, offset_key, plant_key, strength_key = jax.random.split(jax.random.fold_in(key, 11), 4)
    base = jax.random.normal(base_key, (DOCS, D), jnp.float32)
    offsets = jax.random.randint(offset_key, (DOCS,), -(BAND * ROWS), BAND * ROWS + 1)
    source = jnp.clip(jnp.arange(DOCS, dtype=jnp.int32) + offsets, 0, DOCS - 1)
    planted = jax.random.uniform(plant_key, (DOCS,), jnp.float32) < 0.4
    strength = jax.random.uniform(strength_key, (DOCS,), jnp.float32, 0.5, 2.0)
    mixed = base + jnp.where(planted, strength, 0.0)[:, None] * base[source]
    return mixed.astype(jnp.bfloat16)


def touch_ends(array, rng, least, high):
    longest = array.shape.index(max(array.shape))
    spots = []
    for shift in (0, 1):
        where = [jax.random.randint(jax.random.fold_in(rng, axis), (), 0, length) for axis, length in enumerate(array.shape)]
        where[longest] = (where[longest] + shift) % array.shape[longest]
        spots.append(tuple(where))
    return array.at[spots[0]].set(least).at[spots[1]].set(high)


def setup_inputs(seed: int = 0) -> dict:
    arg_keys = jax.random.split(jax.random.key(seed), 4)
    return {
        "embeddings": draw_embeddings(jax.random.fold_in(arg_keys[3], 71), 0),
        "doc_ids": jax.random.permutation(arg_keys[1], DOCS).astype(jnp.int32),
        "valid_counts": touch_ends(jax.random.randint(arg_keys[2], (BLOCKS,), ROWS // 2, ROWS + 1), jax.random.fold_in(arg_keys[2], 1), ROWS // 2, ROWS).astype(jnp.int32),
    }


def normalize(embeddings):
    floats = embeddings.astype(jnp.float32)
    total = lax.optimization_barrier(jnp.sum(floats * floats, axis=-1, keepdims=True))
    return (floats * lax.rsqrt(total + 1e-06)).astype(jnp.bfloat16)

def pair_maxima(unit_left, ids_left, valid_left, unit_right, ids_right, valid_right):
    scores = lax.dot_general(unit_left, unit_right, (((1,), (1,)), ((), ())), preferred_element_type=jnp.float32)
    both = valid_left[:, None] & valid_right[None, :]
    lower = both & (ids_right[None, :] < ids_left[:, None])
    upper = both & (ids_left[:, None] < ids_right[None, :])
    row_best = lax.optimization_barrier(jnp.max(jnp.where(lower, scores, -1.0), axis=1))
    col_best = lax.optimization_barrier(jnp.max(jnp.where(upper, scores, -1.0), axis=0))
    return (row_best, col_best)

def reference(embeddings, doc_ids, valid_counts):
    block_count = valid_counts.shape[0]
    unit_all = normalize(embeddings).reshape(block_count, ROWS, -1)
    ids_all = doc_ids.reshape(block_count, ROWS)
    valid_all = lax.iota(jnp.int32, ROWS)[None, :] < valid_counts[:, None]

    def self_pair(index):
        row_best, col_best = pair_maxima(unit_all[index], ids_all[index], valid_all[index], unit_all[index], ids_all[index], valid_all[index])
        return row_best
    nearest = lax.map(self_pair, jnp.arange(block_count, dtype=jnp.int32))
    for shift_by in range(1, BAND + 1):

        def cross_pair(index):
            other = jnp.minimum(index + shift_by, block_count - 1).astype(jnp.int32)
            exists = index + shift_by < block_count
            return pair_maxima(unit_all[index], ids_all[index], valid_all[index], unit_all[other], ids_all[other], valid_all[other] & exists)
        row_best, col_best = lax.map(cross_pair, jnp.arange(block_count, dtype=jnp.int32))
        filler = jnp.full((shift_by, ROWS), -1.0, jnp.float32)
        col_back = jnp.concatenate([filler, col_best[:block_count - shift_by]], axis=0)
        nearest = jnp.maximum(nearest, jnp.maximum(row_best, col_back))
    return nearest.reshape(-1)
```

```python
import functools

import jax
import jax.numpy as jnp
from jax import lax
from jax.experimental import pallas as pl
from jax.experimental.pallas import tpu as pltpu
from jax.sharding import PartitionSpec as P

BAND = 4
Y = BAND // 2
HEAD = 16
TILE = 256
LANES = 128
AXES = ("row", "col")


class Plan:
    def __init__(self, rows, cols):
        self.R, self.Z, self.C = rows, cols // Y, cols
        Z, R = self.Z, self.R
        even, odd, gate = range(0, R, 2), range(1, R, 2), range(1, R - 1, 2)
        at, ys = self.at, range(Y)
        self.swap_odd = [(at(r, z, y), at(r, z, 1 - y)) for r in odd for z in range(Z) for y in ys]
        self.swap_even = [(at(r, z, y), at(r, z, 1 - y)) for r in even for z in range(Z) for y in ys]
        self.first = [(at(r, z, y), at(r, z - 1, y)) for r in even for z in range(1, Z) for y in ys]
        self.first += [(at(r, z, y), at(r, z + 1, y)) for r in odd for z in range(Z - 1) for y in ys]
        self.second = [(at(r, z, y), at(r, z - 1, y)) for r in even for z in range(1, Z - 1) for y in ys]
        self.second += [(at(r, z, y), at(r, z + 1, y)) for r in odd for z in range(1, Z - 1) for y in ys]
        self.side = [(at(r, 0, y), at(r, 1, y)) for r in odd for y in ys]
        self.side += [(at(r, Z - 1, y), at(r, Z - 2, y)) for r in gate for y in ys]
        self.kin = [(at(r, Z - 4, y), at(r + 1, 0, y)) for r in even for y in ys]
        self.kin += [(at(r, Z - 3, y), at(r + 1, 1, y)) for r in even for y in ys]
        self.across = [(at(r, Z - 1, y), at(r + 1, Z - 1, y)) for r in gate for y in ys]
        self.across += [(at(r + 1, 0, y), at(r, 0, y)) for r in gate for y in ys]
        self.top = [(at(r + 1, Z - 1, y), at(r, Z - 2, y)) for r in gate for y in ys]
        self.gate_a = [(at(r + 1, 0, y), at(r, Z - 2, y)) for r in gate for y in ys]
        self.gate_a += [(at(r, Z - 1, y), at(r + 1, 1, y)) for r in gate for y in ys]
        self.gate_b = [(at(r, 0, y), at(r, Z - 2, y)) for r in gate for y in ys]
        self.gate_b += [(at(r + 1, Z - 1, y), at(r + 1, 1, y)) for r in gate for y in ys]
        self.first_back = [(b, a) for a, b in self.first]
        self.second_back = [(at(r, z, y), at(r, z + 2, y)) for r in even for z in range(Z - 2) for y in ys]
        self.second_back += [(at(r, z, y), at(r, z - 2, y)) for r in odd for z in range(2, Z) for y in ys]
        self.kin_back = [(at(r + 1, 0, y), at(r, Z - 2, y)) for r in even for y in ys]
        self.kin_back += [(at(r + 1, 1, y), at(r, Z - 1, y)) for r in even for y in ys]
        self.side_back = [(at(r, 1, y), at(r, 0, 1 - y)) for r in odd for y in ys]
        self.side_back_late = [(at(r, Z - 2, y), at(r, Z - 1, 1 - y)) for r in gate for y in ys]
        self.top_back = [(at(r, Z - 2, y), at(r, Z - 1, y)) for r in gate for y in ys]
        self.gate_back = [(b, a) for a, b in self.gate_a]
        self.swap = self.swap_even + self.swap_odd
        self.swap_late = [(at(r, Z - 2, y), at(r, Z - 2, 1 - y)) for r in gate for y in ys]
        self.swap_late += [(at(r + 1, 1, y), at(r + 1, 1, 1 - y)) for r in gate for y in ys]

    def at(self, r, z, y):
        return r * self.C + z * Y + y

    def place(self, index):
        r, c = index // self.C, index % self.C
        return r, c // Y, c % Y

    def is_target(self, pairs, index):
        hit = [False] * (self.R * self.C)
        for _, b in pairs:
            hit[b] = True
        return jnp.asarray(hit)[index]


def permute(block, pairs):
    return lax.ppermute(block, AXES, pairs)


def pack_kernel(docs, count_ref, emb_ref, ids_ref, out_ref):
    n = emb_ref.shape[0]
    lane = lax.broadcasted_iota(jnp.int32, (1, n), 1)
    code = jnp.where(lane < count_ref[0], docs - ids_ref[...], 0)
    row = lax.broadcasted_iota(jnp.int32, (HEAD, n), 0)
    head = jnp.where(row == 0, code & 255, jnp.where(row == 1, (code >> 8) & 255, jnp.where(row == 2, code >> 16, 0)))
    out_ref[:HEAD, :n] = head.astype(jnp.float32).astype(jnp.bfloat16)
    if out_ref.shape[1] > n:
        out_ref[:HEAD, n:] = jnp.zeros((HEAD, out_ref.shape[1] - n), jnp.bfloat16)
    step = LANES

    def body(i, _):
        x = emb_ref[pl.ds(pl.multiple_of(i * step, step), step), :].astype(jnp.float32)
        total = jnp.sum(x * x, axis=-1, keepdims=True)
        out_ref[pl.ds(pl.multiple_of(HEAD + i * step, HEAD), step), :] = (x * lax.rsqrt(total + 1e-06)).astype(jnp.bfloat16)
        return 0

    lax.fori_loop(0, n // step, body, 0)


def codes(ref, n):
    head = ref[:HEAD, :n].astype(jnp.float32)
    return head[0:1] + 256.0 * head[1:2] + 65536.0 * head[2:3]


def spread(row, out_ref):
    for g in range(row.shape[1] // LANES):
        block = jnp.broadcast_to(row[:, g * LANES : (g + 1) * LANES], (LANES, LANES))
        out_ref[g * LANES : (g + 1) * LANES, :] = block.T


def gather_rows(acc_ref):
    parts = [
        jnp.max(acc_ref[g * LANES : (g + 1) * LANES, :].T, axis=0, keepdims=True)
        for g in range(acc_ref.shape[0] // LANES)
    ]
    return jnp.concatenate(parts, axis=1)


def pair_job(left_ref, spread_ref, right_ref, right_from, right_codes, row_acc, col_acc, col_from=0):
    n = spread_ref.shape[0]
    count = right_codes.shape[1]
    tiles = [(t, min(TILE, count - t)) for t in range(0, count, TILE)]

    def body(i, _):
        at = pl.multiple_of(i * TILE, TILE)
        left = left_ref[pl.ds(pl.multiple_of(HEAD + i * TILE, HEAD), TILE), :]
        mine = spread_ref[pl.ds(at, TILE), :]
        best = row_acc[pl.ds(at, TILE), :] if row_acc is not None else None
        for t, width in tiles:
            scores = lax.dot_general(
                left,
                right_ref[right_from + t : right_from + t + width, :],
                (((1,), (1,)), ((), ())),
                preferred_element_type=jnp.float32,
            )
            for g in range(0, width, LANES):
                part = scores[:, g : g + LANES]
                lower = right_codes[:, t + g : t + g + LANES] > mine
                if row_acc is not None:
                    best = jnp.maximum(best, jnp.where(lower, part, -1.0))
                if col_acc is not None:
                    up = jnp.where(lower, -1.0, part).reshape(TILE // 8, 8, LANES)
                    spot = slice(col_from + t + g, col_from + t + g + LANES)
                    col_acc[:, spot] = jnp.maximum(col_acc[:, spot], jnp.max(up, axis=0))
        if row_acc is not None:
            row_acc[pl.ds(at, TILE), :] = best
        return 0

    lax.fori_loop(0, n // TILE, body, 0)


def clear(*refs):
    for ref in refs:
        ref[...] = jnp.full(ref.shape, -1.0, jnp.float32)


def put_rows(out_ref, acc_ref):
    out_ref[...] = gather_rows(acc_ref)


def put_cols(out_ref, acc_ref):
    out_ref[...] = jnp.max(acc_ref[...], axis=0, keepdims=True)


def position(plan, index_ref):
    r, z, y = plan.place(index_ref[0])
    return r, z, y, r % 2 == 0


def self_kernel(plan, index_ref, own_ref, own_out, own_codes, own_best):
    n = own_codes.shape[0]
    clear(own_best)
    row = codes(own_ref, n)
    spread(row, own_codes)
    pair_job(own_ref, own_codes, own_ref, HEAD, row, own_best, None)
    put_rows(own_out, own_best)


def first_kernel(plan, index_ref, own_ref, odd_ref, r1_ref, own_out, y_out, r1_out, own_codes, y_codes, own_best, y_best, r1_best):
    n = own_codes.shape[0]
    r, z, y, even = position(plan, index_ref)
    has_r1 = jnp.where(even, z <= plan.Z - 2, z >= 1)
    clear(own_best, y_best, r1_best)
    spread(codes(own_ref, n), own_codes)

    @pl.when(has_r1)
    def _():
        pair_job(own_ref, own_codes, r1_ref, HEAD, codes(r1_ref, n), own_best, r1_best)

    @pl.when(~even)
    def _():
        row = codes(odd_ref, n)
        pair_job(own_ref, own_codes, odd_ref, HEAD, row, own_best, None)
        spread(row, y_codes)

        @pl.when(has_r1)
        def _():
            pair_job(odd_ref, y_codes, r1_ref, HEAD, codes(r1_ref, n), y_best, r1_best)

    put_rows(own_out, own_best)
    put_rows(y_out, y_best)
    put_cols(r1_out, r1_best)


def second_kernel(plan, index_ref, own_ref, even_ref, odd_ref, r1_ref, r2_ref, own_out, y_out, r1_out, r2_out, own_codes, y_codes, own_best, y_best, r1_best, r2_best):
    n = own_codes.shape[0]
    r, z, y, even = position(plan, index_ref)
    has_r1 = jnp.where(even, z <= plan.Z - 2, z >= 1)
    has_r2 = jnp.where(even, z <= plan.Z - 3, z >= 2)
    clear(own_best, y_best, r1_best, r2_best)
    spread(codes(own_ref, n), own_codes)

    @pl.when(has_r2)
    def _():
        pair_job(own_ref, own_codes, r2_ref, HEAD, codes(r2_ref, n), own_best, r2_best)

    @pl.when(even)
    def _():
        row = codes(even_ref, n)
        pair_job(own_ref, own_codes, even_ref, HEAD, row, own_best, None)
        spread(row, y_codes)

        @pl.when(has_r1)
        def _():
            pair_job(even_ref, y_codes, r1_ref, HEAD, codes(r1_ref, n), y_best, r1_best)

        @pl.when(has_r2 & (y == 0))
        def _():
            pair_job(even_ref, y_codes, r2_ref, HEAD, codes(r2_ref, n), y_best, r2_best)

    @pl.when((~even) & has_r2 & (y == 1))
    def _():
        spread(codes(odd_ref, n), y_codes)
        pair_job(odd_ref, y_codes, r2_ref, HEAD, codes(r2_ref, n), y_best, r2_best)

    put_rows(own_out, own_best)
    put_rows(y_out, y_best)
    put_cols(r1_out, r1_best)
    put_cols(r2_out, r2_best)


def kin_kernel(plan, index_ref, own_ref, odd_ref, r1_ref, side_ref, kin_ref, own_out, y_out, r1_out, side_out, kin_out, left_codes, own_best, y_best, r1_best, side_best, kin_best):
    n = left_codes.shape[0]
    r, z, y, even = position(plan, index_ref)
    clear(own_best, y_best, r1_best, side_best, kin_best)

    @pl.when((~even) & (z <= 1))
    def _():
        row = codes(kin_ref, n)
        spread(codes(own_ref, n), left_codes)
        pair_job(own_ref, left_codes, kin_ref, HEAD, row, own_best, kin_best)

        @pl.when(y == 1)
        def _():
            spread(codes(odd_ref, n), left_codes)
            pair_job(odd_ref, left_codes, kin_ref, HEAD, row, y_best, kin_best)

        @pl.when(z == 1)
        def _():
            spread(codes(r1_ref, n), left_codes)
            pair_job(r1_ref, left_codes, kin_ref, HEAD, row, r1_best, kin_best)
            spread(codes(side_ref, n), left_codes)
            pair_job(side_ref, left_codes, kin_ref, HEAD, row, side_best, kin_best)

    put_rows(own_out, own_best)
    put_rows(y_out, y_best)
    put_rows(r1_out, r1_best)
    put_rows(side_out, side_best)
    put_cols(kin_out, kin_best)


def gate_kernel(plan, index_ref, own_ref, even_ref, odd_ref, top_ref, side_ref, ua_ref, ub_ref, own_out, y_out, top_out, side_out, u_out, left_codes, own_best, y_best, top_best, side_best, u_best):
    n = left_codes.shape[0]
    half = n // 2
    r, z, y, even = position(plan, index_ref)
    clear(own_best, y_best, top_best, side_best, u_best)

    def meet(left_ref, best):
        row = codes(ua_ref, n)
        spread(codes(left_ref, n), left_codes)
        pair_job(left_ref, left_codes, ua_ref, HEAD, row[:, :half], best, u_best, 0)
        pair_job(left_ref, left_codes, ub_ref, 0, row[:, half:], best, u_best, half)

    low = (~even) & (z == plan.Z - 2) & (r < plan.R - 1)
    high = even & (z == 1) & (r >= 2)

    @pl.when(low | high)
    def _():
        meet(own_ref, own_best)

    @pl.when(low & (y == 0))
    def _():
        meet(odd_ref, y_best)

    @pl.when(high & (y == 1))
    def _():
        meet(even_ref, y_best)

    @pl.when(low)
    def _():
        meet(top_ref, top_best)
        meet(side_ref, side_best)

    put_rows(own_out, own_best)
    put_rows(y_out, y_best)
    put_rows(top_out, top_best)
    put_rows(side_out, side_best)
    put_cols(u_out, u_best)


def stage(kernel, plan, index, blocks, n, outs, spreads, rows, cols, jobs, name):
    vector = jax.ShapeDtypeStruct((1, n), jnp.float32)
    width = blocks[0].shape[1]
    return pl.pallas_call(
        functools.partial(kernel, plan),
        out_shape=[vector] * outs,
        in_specs=[pl.BlockSpec(memory_space=pltpu.SMEM)] + [pl.BlockSpec(memory_space=pltpu.VMEM)] * len(blocks),
        out_specs=[pl.BlockSpec(memory_space=pltpu.VMEM)] * outs,
        scratch_shapes=[pltpu.VMEM((n, LANES), jnp.float32)] * (spreads + rows) + [pltpu.VMEM((8, n), jnp.float32)] * cols,
        cost_estimate=pl.CostEstimate(flops=2 * n * n * width * jobs, bytes_accessed=2 * n * width * len(blocks), transcendentals=0),
        name=name,
    )(index, *blocks)


def local(plan, docs, embeddings, doc_ids, valid_counts):
    n, width = embeddings.shape
    half = HEAD + n // 2
    index = (lax.axis_index("row") * plan.C + lax.axis_index("col")).astype(jnp.int32)
    at = index.reshape(1)
    own = pl.pallas_call(
        functools.partial(pack_kernel, docs),
        out_shape=jax.ShapeDtypeStruct((HEAD + n, width), jnp.bfloat16),
        in_specs=[pl.BlockSpec(memory_space=pltpu.SMEM)] + [pl.BlockSpec(memory_space=pltpu.VMEM)] * 2,
        out_specs=pl.BlockSpec(memory_space=pltpu.VMEM),
        cost_estimate=pl.CostEstimate(flops=4 * n * width, bytes_accessed=4 * n * width, transcendentals=n),
        name="pack",
    )(valid_counts, embeddings, doc_ids.reshape(1, n))

    r1 = permute(own, plan.first)
    odd = permute(own, plan.swap_odd)
    moved = permute(own, plan.across)
    (own_0,) = stage(self_kernel, plan, at, [own], n, 1, 1, 1, 0, 1, "meet_self")
    r2 = permute(r1, plan.second)
    side = permute(odd, plan.side)
    top = permute(moved, plan.top)
    own_late, _ = lax.optimization_barrier((own, r1))
    even = permute(own_late, plan.swap_even)
    own_1, y_1, r1_1 = stage(first_kernel, plan, at, [own, odd, r1], n, 3, 2, 2, 1, 3, "meet_first")
    kin = permute(r2, plan.kin)
    own_last, moved_last, _ = lax.optimization_barrier((own, moved, r2))
    ua = permute(own_last[:half], plan.gate_a)
    ub = permute(moved_last[half:], plan.gate_b)
    own_2, y_2, r1_2, r2_2 = stage(second_kernel, plan, at, [own, even, odd, r1, r2], n, 4, 2, 2, 2, 4, "meet_second")
    own_3, y_3, r1_3, side_3, kin_3 = stage(kin_kernel, plan, at, [own, odd, r1, side, kin], n, 5, 1, 4, 1, 4, "meet_kin")
    own_4, y_4, top_4, side_4, u_4 = stage(gate_kernel, plan, at, [own, even, odd, top, side, ua, ub], n, 5, 1, 4, 1, 4, "meet_gate")

    def back(best, pairs):
        return jnp.where(plan.is_target(pairs, index), permute(best, pairs), -1.0)

    found = [own_0, own_1, own_2, own_3, own_4]
    found.append(back(r2_2, plan.second_back))
    found.append(back(jnp.maximum(jnp.maximum(r1_1, r1_2), r1_3), plan.first_back))
    found.append(back(jnp.maximum(jnp.maximum(y_1, y_2), y_3), plan.swap))
    found.append(back(side_3, plan.side_back))
    found.append(back(kin_3, plan.kin_back))
    found.append(back(u_4, plan.gate_back))
    found.append(back(top_4, plan.top_back))
    found.append(back(side_4, plan.side_back_late))
    found.append(back(y_4, plan.swap_late))
    nearest = functools.reduce(jnp.maximum, found).reshape(n)
    return jnp.where(lax.iota(jnp.int32, n) < valid_counts[0], nearest, -1.0)


def solution(mesh):
    plan = Plan(mesh.shape["row"], mesh.shape["col"])

    def whole(embeddings, doc_ids, valid_counts):
        step = jax.shard_map(
            functools.partial(local, plan, doc_ids.shape[0]),
            mesh=mesh,
            in_specs=(P(AXES, None), P(AXES), P(AXES)),
            out_specs=P(AXES),
            check_vma=False,
        )
        return step(embeddings, doc_ids, valid_counts)

    return whole
```

```python
import functools

import jax
import jax.numpy as jnp
from jax import lax
from jax.experimental import pallas as pl
from jax.experimental.pallas import tpu as pltpu
from jax.sharding import PartitionSpec as P


BAND = 4
Y = BAND // 2
HEAD = 16
TILE = 256
LANES = 128
AXES = ("row", "col")


class Plan:
    def __init__(self, rows, cols):
        self.R, self.Z, self.C = rows, cols // Y, cols
        Z, R = self.Z, self.R
        even, odd, gate = range(0, R, 2), range(1, R, 2), range(1, R - 1, 2)
        at, ys = self.at, range(Y)
        self.swap_odd = [(at(r, z, y), at(r, z, 1 - y)) for r in odd for z in range(Z) for y in ys]
        self.swap_even = [(at(r, z, y), at(r, z, 1 - y)) for r in even for z in range(Z) for y in ys]
        self.first = [(at(r, z, y), at(r, z - 1, y)) for r in even for z in range(1, Z) for y in ys]
        self.first += [(at(r, z, y), at(r, z + 1, y)) for r in odd for z in range(Z - 1) for y in ys]
        self.second = [(at(r, z, y), at(r, z - 1, y)) for r in even for z in range(1, Z - 1) for y in ys]
        self.second += [(at(r, z, y), at(r, z + 1, y)) for r in odd for z in range(1, Z - 1) for y in ys]
        self.side = [(at(r, 0, y), at(r, 1, y)) for r in odd for y in ys]
        self.side += [(at(r, Z - 1, y), at(r, Z - 2, y)) for r in gate for y in ys]
        self.kin = [(at(r, Z - 4, y), at(r + 1, 0, y)) for r in even for y in ys]
        self.kin += [(at(r, Z - 3, y), at(r + 1, 1, y)) for r in even for y in ys]
        self.across = [(at(r, Z - 1, y), at(r + 1, Z - 1, y)) for r in gate for y in ys]
        self.across += [(at(r + 1, 0, y), at(r, 0, y)) for r in gate for y in ys]
        self.top = [(at(r + 1, Z - 1, y), at(r, Z - 2, y)) for r in gate for y in ys]
        self.gate_a = [(at(r + 1, 0, y), at(r, Z - 2, y)) for r in gate for y in ys]
        self.gate_a += [(at(r, Z - 1, y), at(r + 1, 1, y)) for r in gate for y in ys]
        self.gate_b = [(at(r, 0, y), at(r, Z - 2, y)) for r in gate for y in ys]
        self.gate_b += [(at(r + 1, Z - 1, y), at(r + 1, 1, y)) for r in gate for y in ys]
        self.first_back = [(b, a) for a, b in self.first]
        self.second_back = [(at(r, z, y), at(r, z + 2, y)) for r in even for z in range(Z - 2) for y in ys]
        self.second_back += [(at(r, z, y), at(r, z - 2, y)) for r in odd for z in range(2, Z) for y in ys]
        self.kin_back = [(at(r + 1, 0, y), at(r, Z - 2, y)) for r in even for y in ys]
        self.kin_back += [(at(r + 1, 1, y), at(r, Z - 1, y)) for r in even for y in ys]
        self.side_back = [(at(r, 1, y), at(r, 0, 1 - y)) for r in odd for y in ys]
        self.side_back_late = [(at(r, Z - 2, y), at(r, Z - 1, 1 - y)) for r in gate for y in ys]
        self.top_back = [(at(r, Z - 2, y), at(r, Z - 1, y)) for r in gate for y in ys]
        self.gate_back = [(b, a) for a, b in self.gate_a]
        self.swap = self.swap_even + self.swap_odd
        self.swap_late = [(at(r, Z - 2, y), at(r, Z - 2, 1 - y)) for r in gate for y in ys]
        self.swap_late += [(at(r + 1, 1, y), at(r + 1, 1, 1 - y)) for r in gate for y in ys]

    def at(self, r, z, y):
        return r * self.C + z * Y + y

    def place(self, index):
        r, c = index // self.C, index % self.C
        return r, c // Y, c % Y


def permute(block, pairs):
    return lax.ppermute(block, AXES, pairs)


def pack_kernel(docs, count_ref, emb_ref, ids_ref, out_ref):
    n = emb_ref.shape[0]
    lane = lax.broadcasted_iota(jnp.int32, (1, n), 1)
    code = jnp.where(lane < count_ref[0], docs - ids_ref[...], 0)
    row = lax.broadcasted_iota(jnp.int32, (HEAD, n), 0)
    head = jnp.where(row == 0, code & 255, jnp.where(row == 1, (code >> 8) & 255, jnp.where(row == 2, code >> 16, 0)))
    out_ref[:HEAD, :n] = head.astype(jnp.float32).astype(jnp.bfloat16)
    if out_ref.shape[1] > n:
        out_ref[:HEAD, n:] = jnp.zeros((HEAD, out_ref.shape[1] - n), jnp.bfloat16)
    step = LANES

    def body(i, _):
        x = emb_ref[pl.ds(pl.multiple_of(i * step, step), step), :].astype(jnp.float32)
        total = jnp.sum(x * x, axis=-1, keepdims=True)
        out_ref[pl.ds(pl.multiple_of(HEAD + i * step, HEAD), step), :] = (x * lax.rsqrt(total + 1e-06)).astype(jnp.bfloat16)
        return 0

    lax.fori_loop(0, n // step, body, 0)


def codes(ref, n):
    head = ref[:HEAD, :n].astype(jnp.float32)
    return head[0:1] + 256.0 * head[1:2] + 65536.0 * head[2:3]


def spread(row, out_ref):
    for g in range(row.shape[1] // LANES):
        block = jnp.broadcast_to(row[:, g * LANES : (g + 1) * LANES], (LANES, LANES))
        out_ref[g * LANES : (g + 1) * LANES, :] = block.T


def gather_rows(acc_ref):
    parts = [
        jnp.max(acc_ref[g * LANES : (g + 1) * LANES, :].T, axis=0, keepdims=True)
        for g in range(acc_ref.shape[0] // LANES)
    ]
    return jnp.concatenate(parts, axis=1)


def pair_job(left_ref, spread_ref, right_ref, right_from, right_codes, row_acc, col_acc, scores_ref, col_from=0):
    n = spread_ref.shape[0]
    count = right_codes.shape[1]
    groups = range(0, count, LANES)

    def multiply(i):
        scores_ref[i % 2, :, :count] = lax.dot_general(
            left_ref[HEAD + i * TILE : HEAD + (i + 1) * TILE, :],
            right_ref[right_from : right_from + count, :],
            (((1,), (1,)), ((), ())),
            preferred_element_type=jnp.float32,
        )

    def reduce(i):
        ups = [None] * len(groups)
        theirs = [jnp.broadcast_to(right_codes[:, g : g + LANES], (8, LANES)) for g in groups]
        for j in range(i * TILE, (i + 1) * TILE, 8):
            mine = spread_ref[j : j + 8, :]
            best = row_acc[j : j + 8, :] if row_acc is not None else None
            for k, g in enumerate(groups):
                part = scores_ref[i % 2, j - i * TILE : j - i * TILE + 8, g : g + LANES]
                lower = theirs[k] > mine
                if row_acc is not None:
                    best = jnp.maximum(best, jnp.where(lower, part, -1.0))
                if col_acc is not None:
                    up = jnp.where(lower, -1.0, part)
                    ups[k] = up if ups[k] is None else jnp.maximum(ups[k], up)
            if row_acc is not None:
                row_acc[j : j + 8, :] = best
        if col_acc is not None:
            for k, g in enumerate(groups):
                spot = slice(col_from + g, col_from + g + LANES)
                col_acc[:, spot] = jnp.maximum(col_acc[:, spot], ups[k])

    last = n // TILE - 1
    multiply(0)
    for i in range(1, last + 1):
        multiply(i)
        reduce(i - 1)
    reduce(last)


def clear(*refs):
    for ref in refs:
        ref[...] = jnp.full(ref.shape, -1.0, jnp.float32)


def put_rows(out_ref, acc_ref, *so_far):
    found = gather_rows(acc_ref)
    for ref in so_far:
        found = jnp.maximum(found, ref[...])
    out_ref[...] = found


def put_cols(out_ref, acc_ref, *so_far):
    found = jnp.max(acc_ref[...], axis=0, keepdims=True)
    for ref in so_far:
        found = jnp.maximum(found, ref[...])
    out_ref[...] = found


class Fetch:
    def __init__(self, needed, source, target, sem):
        self.needed, self.target = needed, target
        self.copy = pltpu.make_async_copy(source, target, sem)

    def start(self):
        if self.needed is True:
            self.copy.start()
        else:
            pl.when(self.needed)(self.copy.start)

    def wait(self):
        if self.needed is True:
            self.copy.wait()
        else:
            pl.when(self.needed)(self.copy.wait)
        return self.target


def fetches(refs, held, sems, needed):
    out = [Fetch(c, ref, h, sems.at[i]) for i, (ref, h, c) in enumerate(zip(refs, held, needed))]
    for f in out:
        f.start()
    return out


def position(plan, index_ref):
    index = index_ref[0]
    r, c = index // plan.C, index % plan.C
    return r, c // Y, c % Y, r % 2 == 0


def self_kernel(plan, index_ref, own_hbm, own_out, own_v, sems, scores, own_codes, own_best):
    n = own_codes.shape[0]
    (own,) = fetches([own_hbm], [own_v], sems, [True])
    clear(own_best)
    own = own.wait()
    row = codes(own, n)
    spread(row, own_codes)
    pair_job(own, own_codes, own, HEAD, row, own_best, None, scores)
    put_rows(own_out, own_best)


def first_kernel(plan, index_ref, own_hbm, r1_hbm, odd_hbm, own_out, y_out, r1_out, own_v, r1_v, odd_v, sems, scores, own_codes, y_codes, own_best, y_best, r1_best):
    n = own_codes.shape[0]
    _, z, _, even = position(plan, index_ref)
    has_r1 = jnp.where(even, z <= plan.Z - 2, z >= 1)
    own, r1, odd = fetches([own_hbm, r1_hbm, odd_hbm], [own_v, r1_v, odd_v], sems, [True, has_r1, ~even])
    clear(own_best, y_best, r1_best)
    own = own.wait()
    spread(codes(own, n), own_codes)
    r1 = r1.wait()

    @pl.when(has_r1)
    def _():
        pair_job(own, own_codes, r1, HEAD, codes(r1, n), own_best, r1_best, scores)

    held = odd.wait()

    @pl.when(~even)
    def _():
        row = codes(held, n)
        pair_job(own, own_codes, held, HEAD, row, own_best, None, scores)
        spread(row, y_codes)

    @pl.when((~even) & has_r1)
    def _():
        pair_job(held, y_codes, r1, HEAD, codes(r1, n), y_best, r1_best, scores)

    put_rows(own_out, own_best)
    put_rows(y_out, y_best)
    put_cols(r1_out, r1_best)


def second_kernel(plan, index_ref, own_hbm, r2_hbm, even_hbm, r1_hbm, odd_hbm, y_in, r1_in, own_out, y_out, r1_out, r2_out, own_v, r2_v, y_v, r1_v, sems, scores, own_codes, y_codes, own_best, y_best, r1_best, r2_best):
    n = own_codes.shape[0]
    _, z, y, even = position(plan, index_ref)
    has_r1 = even & (z <= plan.Z - 2)
    has_r2 = jnp.where(even, z <= plan.Z - 3, z >= 2)
    late_y = (~even) & has_r2 & (y == 1)
    own, r2, lower, r1, upper = fetches(
        [own_hbm, r2_hbm, even_hbm, r1_hbm, odd_hbm], [own_v, r2_v, y_v, r1_v, y_v], sems, [True, has_r2, even, has_r1, late_y]
    )
    clear(own_best, y_best, r1_best, r2_best)
    own = own.wait()
    spread(codes(own, n), own_codes)
    r2 = r2.wait()

    @pl.when(has_r2)
    def _():
        pair_job(own, own_codes, r2, HEAD, codes(r2, n), own_best, r2_best, scores)

    held = lower.wait()
    upper.wait()

    @pl.when(even)
    def _():
        pair_job(own, own_codes, held, HEAD, codes(held, n), own_best, None, scores)

    @pl.when(even | late_y)
    def _():
        spread(codes(held, n), y_codes)

    @pl.when((even & has_r2 & (y == 0)) | late_y)
    def _():
        pair_job(held, y_codes, r2, HEAD, codes(r2, n), y_best, r2_best, scores)

    r1 = r1.wait()

    @pl.when(has_r1)
    def _():
        pair_job(held, y_codes, r1, HEAD, codes(r1, n), y_best, r1_best, scores)

    put_rows(own_out, own_best)
    put_rows(y_out, y_best, y_in)
    put_cols(r1_out, r1_best, r1_in)
    put_cols(r2_out, r2_best)


def kin_kernel(plan, index_ref, own_hbm, kin_hbm, r1_hbm, side_hbm, odd_hbm, y_in, r1_in, own_out, y_out, r1_out, side_out, kin_out, own_v, kin_v, r1_v, side_v, odd_v, sems, scores, left_codes, own_best, y_best, r1_best, side_best, kin_best):
    n = left_codes.shape[0]
    _, z, y, even = position(plan, index_ref)
    here = (~even) & (z <= 1)
    both = (~even) & (z == 1)
    cross = here & (y == 1)
    own, kin, r1, side, odd = fetches(
        [own_hbm, kin_hbm, r1_hbm, side_hbm, odd_hbm], [own_v, kin_v, r1_v, side_v, odd_v], sems, [here, here, both, both, cross]
    )
    clear(own_best, y_best, r1_best, side_best, kin_best)
    own, kin = own.wait(), kin.wait()

    def meet(left, best):
        spread(codes(left, n), left_codes)
        pair_job(left, left_codes, kin, HEAD, codes(kin, n), best, kin_best, scores)

    @pl.when(here)
    def _():
        meet(own, own_best)

    r1, side = r1.wait(), side.wait()

    @pl.when(both)
    def _():
        meet(r1, r1_best)
        meet(side, side_best)

    odd = odd.wait()

    @pl.when(cross)
    def _():
        meet(odd, y_best)

    put_rows(own_out, own_best)
    put_rows(y_out, y_best, y_in)
    put_rows(r1_out, r1_best, r1_in)
    put_rows(side_out, side_best)
    put_cols(kin_out, kin_best)


def gate_kernel(plan, index_ref, own_hbm, ua_hbm, ub_hbm, top_hbm, side_hbm, even_hbm, odd_hbm, own_out, y_out, top_out, side_out, u_out, own_v, ua_v, ub_v, top_v, side_v, y_v, sems, scores, left_codes, own_best, y_best, top_best, side_best, u_best):
    n = left_codes.shape[0]
    half = n // 2
    r, z, y, even = position(plan, index_ref)
    low = (~even) & (z == plan.Z - 2) & (r < plan.R - 1)
    high = even & (z == 1) & (r >= 2)
    here = low | high
    own, ua, ub, top, side, lower, upper = fetches(
        [own_hbm, ua_hbm, ub_hbm, top_hbm, side_hbm, even_hbm, odd_hbm],
        [own_v, ua_v, ub_v, top_v, side_v, y_v, y_v],
        sems,
        [here, here, here, low, low, high & (y == 1), low & (y == 0)],
    )
    clear(own_best, y_best, top_best, side_best, u_best)
    own, ua, ub = own.wait(), ua.wait(), ub.wait()

    def meet(left, best):
        row = codes(ua, n)
        spread(codes(left, n), left_codes)
        pair_job(left, left_codes, ua, HEAD, row[:, :half], best, u_best, scores, 0)
        pair_job(left, left_codes, ub, 0, row[:, half:], best, u_best, scores, half)

    @pl.when(here)
    def _():
        meet(own, own_best)

    top, side = top.wait(), side.wait()

    @pl.when(low)
    def _():
        meet(top, top_best)
        meet(side, side_best)

    held = lower.wait()
    upper.wait()

    @pl.when((high & (y == 1)) | (low & (y == 0)))
    def _():
        meet(held, y_best)

    put_rows(own_out, own_best)
    put_rows(y_out, y_best)
    put_rows(top_out, top_best)
    put_rows(side_out, side_best)
    put_cols(u_out, u_best)


def finish_kernel(plan, index_ref, count_ref, own_0, own_1, own_2, own_3, own_4, second, first, swap, side, kin, gate, top, side_late, swap_late, out_ref):
    r, z, _, even = position(plan, index_ref)
    Z, R = plan.Z, plan.R
    found = functools.reduce(jnp.maximum, [ref[...] for ref in (own_0, own_1, own_2, own_3, own_4, swap)])
    inner = (~even) & (r < R - 1)
    returns = (
        (second, jnp.where(even, z >= 2, z <= Z - 3)),
        (first, jnp.where(even, z >= 1, z <= Z - 2)),
        (side, (~even) & (z == 0)),
        (kin, even & (z >= Z - 2)),
        (gate, (even & (r >= 2) & (z == 0)) | (inner & (z == Z - 1))),
        (top, inner & (z == Z - 1)),
        (side_late, inner & (z == Z - 1)),
        (swap_late, (inner & (z == Z - 2)) | (even & (r >= 2) & (z == 1))),
    )
    for ref, mine in returns:
        found = jnp.maximum(found, jnp.where(mine, ref[...], -1.0))
    lane = lax.broadcasted_iota(jnp.int32, found.shape, 1)
    out_ref[...] = jnp.where(lane < count_ref[0], found, -1.0)


SMEM, VMEM, ANY = (pl.BlockSpec(memory_space=m) for m in (pltpu.SMEM, pltpu.VMEM, pl.ANY))


def stage(kernel, plan, index, blocks, vectors, n, outs, spreads, rows, cols, jobs, held=None):
    vector = jax.ShapeDtypeStruct((1, n), jnp.float32)
    width = blocks[0].shape[1]
    held = blocks if held is None else held
    scratch = [pltpu.VMEM(b.shape, b.dtype) for b in held] + [pltpu.SemaphoreType.DMA((len(blocks),)), pltpu.VMEM((2, TILE, n), jnp.float32)]
    scratch += [pltpu.VMEM((n, LANES), jnp.float32)] * (spreads + rows) + [pltpu.VMEM((8, n), jnp.float32)] * cols
    return pl.pallas_call(
        functools.partial(kernel, plan),
        out_shape=[vector] * outs,
        in_specs=[SMEM] + [ANY] * len(blocks) + [VMEM] * len(vectors),
        out_specs=[VMEM] * outs,
        scratch_shapes=scratch,
        cost_estimate=pl.CostEstimate(flops=2 * n * n * width * jobs, bytes_accessed=2 * n * width * len(blocks), transcendentals=0),
    )(index, *blocks, *vectors)


def local(plan, docs, embeddings, doc_ids, valid_counts):
    return body(plan, docs, embeddings, doc_ids, valid_counts)


def body(plan, docs, embeddings, doc_ids, valid_counts):
    n, width = embeddings.shape
    half = HEAD + n // 2
    at = (lax.axis_index("row") * plan.C + lax.axis_index("col")).astype(jnp.int32).reshape(1)
    own = pl.pallas_call(
        functools.partial(pack_kernel, docs),
        out_shape=jax.ShapeDtypeStruct((HEAD + n, width), jnp.bfloat16),
        in_specs=[SMEM, VMEM, VMEM],
        out_specs=VMEM,
        cost_estimate=pl.CostEstimate(flops=4 * n * width, bytes_accessed=4 * n * width, transcendentals=n),
        name="pack",
    )(valid_counts, embeddings, doc_ids.reshape(1, n))

    r1 = permute(own, plan.first)
    odd = permute(own, plan.swap_odd)
    moved = permute(own, plan.across)
    (own_0,) = stage(self_kernel, plan, at, [own], [], n, 1, 1, 1, 0, 1)
    own_a, moved_b = own[:half], moved[half:]
    r2 = permute(r1, plan.second)
    side = permute(odd, plan.side)
    top = permute(moved, plan.top)
    own_late, _ = lax.optimization_barrier((own, r1))
    even = permute(own_late, plan.swap_even)
    own_1, y_1, r1_1 = stage(first_kernel, plan, at, [own, r1, odd], [], n, 3, 2, 2, 1, 3)
    kin = permute(r2, plan.kin)
    own_a, moved_b, _ = lax.optimization_barrier((own_a, moved_b, r2))
    ua = permute(own_a, plan.gate_a)
    ub = permute(moved_b, plan.gate_b)
    own_2, y_2, r1_2, r2_2 = stage(second_kernel, plan, at, [own, r2, even, r1, odd], [y_1, r1_1], n, 4, 2, 2, 2, 4, held=[own, r2, even, r1])
    own_3, y_3, r1_3, side_3, kin_3 = stage(kin_kernel, plan, at, [own, kin, r1, side, odd], [y_2, r1_2], n, 5, 1, 4, 1, 4)
    own_4, y_4, top_4, side_4, u_4 = stage(gate_kernel, plan, at, [own, ua, ub, top, side, even, odd], [], n, 5, 1, 4, 1, 4, held=[own, ua, ub, top, side, even])

    returned = [
        permute(r2_2, plan.second_back),
        permute(r1_3, plan.first_back),
        permute(y_3, plan.swap),
        permute(side_3, plan.side_back),
        permute(kin_3, plan.kin_back),
        permute(u_4, plan.gate_back),
        permute(top_4, plan.top_back),
        permute(side_4, plan.side_back_late),
        permute(y_4, plan.swap_late),
    ]
    nearest = pl.pallas_call(
        functools.partial(finish_kernel, plan),
        out_shape=jax.ShapeDtypeStruct((1, n), jnp.float32),
        in_specs=[SMEM, SMEM] + [VMEM] * 14,
        out_specs=VMEM,
        name="finish",
    )(at, valid_counts, own_0, own_1, own_2, own_3, own_4, *returned)
    return nearest.reshape(n)


def solution(mesh):
    plan = Plan(mesh.shape["row"], mesh.shape["col"])

    def whole(embeddings, doc_ids, valid_counts):
        step = jax.shard_map(
            functools.partial(local, plan, doc_ids.shape[0]),
            mesh=mesh,
            in_specs=(P(AXES, None), P(AXES), P(AXES)),
            out_specs=P(AXES),
            check_vma=False,
        )
        return step(embeddings, doc_ids, valid_counts)

    return whole
```

```python
import functools
import math

import jax
import jax.numpy as jnp
from jax import lax
from jax.experimental import pallas as pl
from jax.experimental.pallas import tpu as pltpu
from jax.sharding import PartitionSpec as P


BAND = 4
Y = BAND // 2
HEAD = 16
TILE = 384
LANES = 128
PARTS = 6
SPARE = 4 << 20
AXES = ("row", "col")


class Plan:
    def __init__(self, rows, cols):
        self.R, self.Z, self.C = rows, cols // Y, cols
        Z, R = self.Z, self.R
        even, odd, gate = range(0, R, 2), range(1, R, 2), range(1, R - 1, 2)
        at, ys = self.at, range(Y)
        self.swap_odd = [(at(r, z, y), at(r, z, 1 - y)) for r in odd for z in range(Z) for y in ys]
        self.swap_even = [(at(r, z, y), at(r, z, 1 - y)) for r in even for z in range(Z) for y in ys]
        self.first = [(at(r, z, y), at(r, z - 1, y)) for r in even for z in range(1, Z) for y in ys]
        self.first += [(at(r, z, y), at(r, z + 1, y)) for r in odd for z in range(Z - 1) for y in ys]
        self.second = [(at(r, z, y), at(r, z - 1, y)) for r in even for z in range(1, Z - 1) for y in ys]
        self.second += [(at(r, z, y), at(r, z + 1, y)) for r in odd for z in range(1, Z - 1) for y in ys]
        self.side = [(at(r, 0, y), at(r, 1, y)) for r in odd for y in ys]
        self.side += [(at(r, Z - 1, y), at(r, Z - 2, y)) for r in gate for y in ys]
        self.kin = [(at(r, Z - 4, y), at(r + 1, 0, y)) for r in even for y in ys]
        self.kin += [(at(r, Z - 3, y), at(r + 1, 1, y)) for r in even for y in ys]
        self.across = [(at(r, Z - 1, y), at(r + 1, Z - 1, y)) for r in gate for y in ys]
        self.across += [(at(r + 1, 0, y), at(r, 0, y)) for r in gate for y in ys]
        self.top = [(at(r + 1, Z - 1, y), at(r, Z - 2, y)) for r in gate for y in ys]
        self.gate_a = [(at(r + 1, 0, y), at(r, Z - 2, y)) for r in gate for y in ys]
        self.gate_a += [(at(r, Z - 1, y), at(r + 1, 1, y)) for r in gate for y in ys]
        self.gate_b = [(at(r, 0, y), at(r, Z - 2, y)) for r in gate for y in ys]
        self.gate_b += [(at(r + 1, Z - 1, y), at(r + 1, 1, y)) for r in gate for y in ys]
        self.first_back = [(b, a) for a, b in self.first]
        self.second_back = [(at(r, z, y), at(r, z + 2, y)) for r in even for z in range(Z - 2) for y in ys]
        self.second_back += [(at(r, z, y), at(r, z - 2, y)) for r in odd for z in range(2, Z) for y in ys]
        self.kin_back = [(at(r + 1, 0, y), at(r, Z - 2, y)) for r in even for y in ys]
        self.kin_back += [(at(r + 1, 1, y), at(r, Z - 1, y)) for r in even for y in ys]
        self.side_back = [(at(r, 1, y), at(r, 0, 1 - y)) for r in odd for y in ys]
        self.side_back_late = [(at(r, Z - 2, y), at(r, Z - 1, 1 - y)) for r in gate for y in ys]
        self.top_back = [(at(r, Z - 2, y), at(r, Z - 1, y)) for r in gate for y in ys]
        self.gate_back = [(b, a) for a, b in self.gate_a]
        self.swap = self.swap_even + self.swap_odd
        self.swap_late = [(at(r, Z - 2, y), at(r, Z - 2, 1 - y)) for r in gate for y in ys]
        self.swap_late += [(at(r + 1, 1, y), at(r + 1, 1, 1 - y)) for r in gate for y in ys]

    def at(self, r, z, y):
        return r * self.C + z * Y + y

    def place(self, index):
        r, c = index // self.C, index % self.C
        return r, c // Y, c % Y


def permute(block, pairs):
    return lax.ppermute(block, AXES, pairs)


def pack_kernel(docs, count_ref, emb_hbm, ids_ref, out_hbm, emb, out, in_sems, out_sems):
    n, width = emb_hbm.shape
    steps = in_sems.shape[0]
    size = n // steps

    def taken(i):
        rows = pl.ds(i * size, size)
        return pltpu.make_async_copy(emb_hbm.at[rows], emb.at[rows], in_sems.at[i])

    def given(i):
        rows = pl.ds(HEAD + i * size, size) if i < steps else pl.ds(0, HEAD)
        return pltpu.make_async_copy(out.at[rows], out_hbm.at[rows], out_sems.at[i])

    for i in range(steps):
        taken(i).start()
    lane = lax.broadcasted_iota(jnp.int32, (1, n), 1)
    code = jnp.where(lane < count_ref[0], docs - ids_ref[...].reshape(1, n), 0)
    row = lax.broadcasted_iota(jnp.int32, (HEAD, n), 0)
    head = jnp.where(row == 0, code & 255, jnp.where(row == 1, (code >> 8) & 255, jnp.where(row == 2, code >> 16, 0)))
    out[:HEAD, :n] = head.astype(jnp.float32).astype(jnp.bfloat16)
    if width > n:
        out[:HEAD, n:] = jnp.zeros((HEAD, width - n), jnp.bfloat16)
    given(steps).start()
    part = 32
    for i in range(steps):
        taken(i).wait()

        def scale(j, _):
            at = i * size + j * part
            x = emb[pl.ds(pl.multiple_of(at, HEAD), part), :].astype(jnp.float32)
            total = jnp.sum(x * x, axis=-1, keepdims=True)
            out[pl.ds(pl.multiple_of(HEAD + at, HEAD), part), :] = (x * lax.rsqrt(total + 1e-06)).astype(jnp.bfloat16)
            return 0

        lax.fori_loop(0, size // part, scale, 0, unroll=True)
        given(i).start()
    for i in range(steps + 1):
        given(i).wait()


def codes(ref, n):
    head = ref[:HEAD, :n].astype(jnp.float32)
    return head[0:1] + 256.0 * head[1:2] + 65536.0 * head[2:3]


def spread(row, out_ref):
    for g in range(row.shape[1] // LANES):
        block = jnp.broadcast_to(row[:, g * LANES : (g + 1) * LANES], (LANES, LANES))
        out_ref[g * LANES : (g + 1) * LANES, :] = block.T


def gather_rows(acc_ref):
    parts = [
        jnp.max(acc_ref[g * LANES : (g + 1) * LANES, :].T, axis=0, keepdims=True)
        for g in range(acc_ref.shape[0] // LANES)
    ]
    return jnp.concatenate(parts, axis=1)


def pair_job(left_ref, left_from, spread_ref, right_ref, right_codes, row_acc, col_acc, scores_ref, rows=None):
    start, stop = rows or (0, spread_ref.shape[0])
    n = right_codes.shape[1]
    groups = range(0, n, LANES)
    tiles = range((stop - start) // TILE)

    def multiply(i):
        scores_ref[i % 2] = lax.dot_general(
            left_ref[left_from + i * TILE : left_from + (i + 1) * TILE, :],
            right_ref[HEAD : HEAD + n, :],
            (((1,), (1,)), ((), ())),
            preferred_element_type=jnp.float32,
        )

    def reduce(i):
        ups = [None] * len(groups)
        theirs = [jnp.broadcast_to(right_codes[:, g : g + LANES], (8, LANES)) for g in groups]
        for j in range(0, TILE, 8):
            at = start + i * TILE + j
            mine = spread_ref[at : at + 8, :]
            best = row_acc[at : at + 8, :]
            for k, g in enumerate(groups):
                part = scores_ref[i % 2, j : j + 8, g : g + LANES]
                lower = theirs[k] > mine
                best = jnp.maximum(best, jnp.where(lower, part, -1.0))
                if col_acc is not None:
                    up = jnp.where(lower, -1.0, part)
                    ups[k] = up if ups[k] is None else jnp.maximum(ups[k], up)
            row_acc[at : at + 8, :] = best
        if col_acc is not None:
            for k, g in enumerate(groups):
                col_acc[:, g : g + LANES] = jnp.maximum(col_acc[:, g : g + LANES], ups[k])

    for i in tiles:
        multiply(i)
        if i > 0:
            reduce(i - 1)
    reduce(tiles[-1])


def clear(*refs):
    for ref in refs:
        ref[...] = jnp.full(ref.shape, -1.0, jnp.float32)


def put_rows(out_ref, acc_ref, *so_far):
    found = gather_rows(acc_ref)
    for ref in so_far:
        found = jnp.maximum(found, ref[...])
    out_ref[...] = found


def put_cols(out_ref, acc_ref, *so_far):
    found = jnp.max(acc_ref[...], axis=0, keepdims=True)
    for ref in so_far:
        found = jnp.maximum(found, ref[...])
    out_ref[...] = found


class Fetch:
    def __init__(self, needed, source, target, sem):
        self.needed, self.target = needed, target
        self.copy = pltpu.make_async_copy(source, target, sem)

    def start(self):
        if self.needed is True:
            self.copy.start()
        else:
            pl.when(self.needed)(self.copy.start)

    def wait(self):
        if self.needed is True:
            self.copy.wait()
        else:
            pl.when(self.needed)(self.copy.wait)
        return self.target


def fetches(refs, held, sems, needed):
    out = [Fetch(c, ref, h, sems.at[i]) for i, (ref, h, c) in enumerate(zip(refs, held, needed))]
    for f in out:
        f.start()
    return out


def position(plan, index_ref):
    index = index_ref[0]
    r, c = index // plan.C, index % plan.C
    return r, c // Y, c % Y, r % 2 == 0


def self_kernel(plan, index_ref, own_hbm, own_out, own_v, sems, scores, own_codes, own_best):
    n = own_codes.shape[0]
    (own,) = fetches([own_hbm], [own_v], sems, [True])
    clear(own_best)
    own = own.wait()
    row = codes(own, n)
    spread(row, own_codes)
    pair_job(own, HEAD, own_codes, own, row, own_best, None, scores)
    put_rows(own_out, own_best)


def first_kernel(plan, index_ref, own_hbm, r1_hbm, odd_hbm, own_out, y_out, r1_out, own_v, r1_v, odd_v, sems, scores, own_codes, y_codes, own_best, y_best, r1_best):
    n = own_codes.shape[0]
    _, z, _, even = position(plan, index_ref)
    has_r1 = jnp.where(even, z <= plan.Z - 2, z >= 1)
    own, r1, odd = fetches([own_hbm, r1_hbm, odd_hbm], [own_v, r1_v, odd_v], sems, [True, has_r1, ~even])
    clear(own_best, y_best, r1_best)
    own = own.wait()
    spread(codes(own, n), own_codes)
    r1 = r1.wait()

    @pl.when(has_r1)
    def _():
        pair_job(own, HEAD, own_codes, r1, codes(r1, n), own_best, r1_best, scores)

    held = odd.wait()

    @pl.when(~even)
    def _():
        row = codes(held, n)
        pair_job(own, HEAD, own_codes, held, row, own_best, None, scores)
        spread(row, y_codes)

    @pl.when((~even) & has_r1)
    def _():
        pair_job(held, HEAD, y_codes, r1, codes(r1, n), y_best, r1_best, scores)

    put_rows(own_out, own_best)
    put_rows(y_out, y_best)
    put_cols(r1_out, r1_best)


def second_kernel(plan, index_ref, own_hbm, r2_hbm, even_hbm, r1_hbm, odd_hbm, y_in, r1_in, own_out, y_out, r1_out, r2_out, own_v, r2_v, y_v, r1_v, sems, scores, own_codes, y_codes, own_best, y_best, r1_best, r2_best):
    n = own_codes.shape[0]
    _, z, y, even = position(plan, index_ref)
    has_r1 = even & (z <= plan.Z - 2)
    has_r2 = jnp.where(even, z <= plan.Z - 3, z >= 2)
    late_y = (~even) & has_r2 & (y == 1)
    own, r2, lower, r1, upper = fetches(
        [own_hbm, r2_hbm, even_hbm, r1_hbm, odd_hbm], [own_v, r2_v, y_v, r1_v, y_v], sems, [True, has_r2, even, has_r1, late_y]
    )
    clear(own_best, y_best, r1_best, r2_best)
    own = own.wait()
    spread(codes(own, n), own_codes)
    r2 = r2.wait()

    @pl.when(has_r2)
    def _():
        pair_job(own, HEAD, own_codes, r2, codes(r2, n), own_best, r2_best, scores)

    held = lower.wait()
    upper.wait()

    @pl.when(even)
    def _():
        pair_job(own, HEAD, own_codes, held, codes(held, n), own_best, None, scores)

    @pl.when(even | late_y)
    def _():
        spread(codes(held, n), y_codes)

    @pl.when((even & has_r2 & (y == 0)) | late_y)
    def _():
        pair_job(held, HEAD, y_codes, r2, codes(r2, n), y_best, r2_best, scores)

    r1 = r1.wait()

    @pl.when(has_r1)
    def _():
        pair_job(held, HEAD, y_codes, r1, codes(r1, n), y_best, r1_best, scores)

    put_rows(own_out, own_best)
    put_rows(y_out, y_best, y_in)
    put_cols(r1_out, r1_best, r1_in)
    put_cols(r2_out, r2_best)


def kin_kernel(plan, index_ref, own_hbm, kin_hbm, r1_hbm, side_hbm, odd_hbm, y_in, r1_in, own_out, y_out, r1_out, side_out, kin_out, own_v, kin_v, r1_v, side_v, odd_v, sems, scores, left_codes, own_best, y_best, r1_best, side_best, kin_best):
    n = left_codes.shape[0]
    _, z, y, even = position(plan, index_ref)
    here = (~even) & (z <= 1)
    both = (~even) & (z == 1)
    cross = here & (y == 1)
    own, kin, r1, side, odd = fetches(
        [own_hbm, kin_hbm, r1_hbm, side_hbm, odd_hbm], [own_v, kin_v, r1_v, side_v, odd_v], sems, [here, here, both, both, cross]
    )
    clear(own_best, y_best, r1_best, side_best, kin_best)
    own, kin = own.wait(), kin.wait()

    def meet(left, best):
        spread(codes(left, n), left_codes)
        pair_job(left, HEAD, left_codes, kin, codes(kin, n), best, kin_best, scores)

    @pl.when(here)
    def _():
        meet(own, own_best)

    r1, side = r1.wait(), side.wait()

    @pl.when(both)
    def _():
        meet(r1, r1_best)
        meet(side, side_best)

    odd = odd.wait()

    @pl.when(cross)
    def _():
        meet(odd, y_best)

    put_rows(own_out, own_best)
    put_rows(y_out, y_best, y_in)
    put_rows(r1_out, r1_best, r1_in)
    put_rows(side_out, side_best)
    put_cols(kin_out, kin_best)


def gate_kernel(plan, index_ref, own_hbm, ua_hbm, ub_hbm, top_hbm, side_hbm, even_hbm, odd_hbm, own_out, y_out, top_out, side_out, u_out, own_v, ua_v, ub_v, top_v, side_v, y_v, sems, scores, u_codes, u_best, own_best, y_best, top_best, side_best):
    n = u_codes.shape[0]
    half = n // 2
    r, z, y, even = position(plan, index_ref)
    low = (~even) & (z == plan.Z - 2) & (r < plan.R - 1)
    high = even & (z == 1) & (r >= 2)
    here = low | high
    own, ua, ub, top, side, lower, upper = fetches(
        [own_hbm, ua_hbm, ub_hbm, top_hbm, side_hbm, even_hbm, odd_hbm],
        [own_v, ua_v, ub_v, top_v, side_v, y_v, y_v],
        sems,
        [here, here, here, low, low, high & (y == 1), low & (y == 0)],
    )
    clear(own_best, y_best, top_best, side_best, u_best)
    own, ua, ub = own.wait(), ua.wait(), ub.wait()

    def meet(right, best):
        row = codes(right, n)
        pair_job(ua, HEAD, u_codes, right, row, u_best, best, scores, (0, half))
        pair_job(ub, 0, u_codes, right, row, u_best, best, scores, (half, n))

    @pl.when(here)
    def _():
        spread(codes(ua, n), u_codes)
        meet(own, own_best)

    top, side = top.wait(), side.wait()

    @pl.when(low)
    def _():
        meet(top, top_best)
        meet(side, side_best)

    held = lower.wait()
    upper.wait()

    @pl.when((high & (y == 1)) | (low & (y == 0)))
    def _():
        meet(held, y_best)

    put_cols(own_out, own_best)
    put_cols(y_out, y_best)
    put_cols(top_out, top_best)
    put_cols(side_out, side_best)
    put_rows(u_out, u_best)


def finish_kernel(plan, index_ref, count_ref, own_0, own_1, own_2, own_3, own_4, second, first, swap, side, kin, gate, top, side_late, swap_late, out_ref):
    r, z, _, even = position(plan, index_ref)
    Z, R = plan.Z, plan.R
    found = functools.reduce(jnp.maximum, [ref[...] for ref in (own_0, own_1, own_2, own_3, own_4, swap)])
    inner = (~even) & (r < R - 1)
    returns = (
        (second, jnp.where(even, z >= 2, z <= Z - 3)),
        (first, jnp.where(even, z >= 1, z <= Z - 2)),
        (side, (~even) & (z == 0)),
        (kin, even & (z >= Z - 2)),
        (gate, (even & (r >= 2) & (z == 0)) | (inner & (z == Z - 1))),
        (top, inner & (z == Z - 1)),
        (side_late, inner & (z == Z - 1)),
        (swap_late, (inner & (z == Z - 2)) | (even & (r >= 2) & (z == 1))),
    )
    for ref, mine in returns:
        found = jnp.maximum(found, jnp.where(mine, ref[...], -1.0))
    lane = lax.broadcasted_iota(jnp.int32, found.shape, 1)
    out_ref[...] = jnp.where(lane < count_ref[0], found, -1.0).reshape(out_ref.shape)


SMEM, VMEM, ANY = (pl.BlockSpec(memory_space=m) for m in (pltpu.SMEM, pltpu.VMEM, pl.ANY))


def stage(kernel, plan, index, blocks, vectors, n, outs, spreads, rows, cols, jobs, held=None):
    vector = jax.ShapeDtypeStruct((1, n), jnp.float32)
    width = blocks[0].shape[1]
    held = blocks if held is None else held
    scratch = [pltpu.VMEM(b.shape, b.dtype) for b in held] + [pltpu.SemaphoreType.DMA((len(blocks),)), pltpu.VMEM((2, TILE, n), jnp.float32)]
    scratch += [pltpu.VMEM((n, LANES), jnp.float32)] * (spreads + rows) + [pltpu.VMEM((8, n), jnp.float32)] * cols
    used = sum(math.prod(b.shape) * 2 for b in held) + 4 * n * (2 * TILE + LANES * (spreads + rows) + 8 * cols)
    return pl.pallas_call(
        functools.partial(kernel, plan),
        compiler_params=pltpu.CompilerParams(vmem_limit_bytes=used + SPARE),
        out_shape=[vector] * outs,
        in_specs=[SMEM] + [ANY] * len(blocks) + [VMEM] * len(vectors),
        out_specs=[VMEM] * outs,
        scratch_shapes=scratch,
        cost_estimate=pl.CostEstimate(flops=2 * n * n * width * jobs, bytes_accessed=2 * n * width * len(blocks), transcendentals=0),
    )(index, *blocks, *vectors)


def local(plan, docs, embeddings, doc_ids, valid_counts):
    return body(plan, docs, embeddings, doc_ids, valid_counts)


def body(plan, docs, embeddings, doc_ids, valid_counts):
    n, width = embeddings.shape
    half = HEAD + n // 2
    at = (lax.axis_index("row") * plan.C + lax.axis_index("col")).astype(jnp.int32).reshape(1)
    own = pl.pallas_call(
        functools.partial(pack_kernel, docs),
        out_shape=jax.ShapeDtypeStruct((HEAD + n, width), jnp.bfloat16),
        in_specs=[SMEM, ANY, VMEM],
        out_specs=ANY,
        scratch_shapes=[
            pltpu.VMEM((n, width), jnp.bfloat16),
            pltpu.VMEM((HEAD + n, width), jnp.bfloat16),
            pltpu.SemaphoreType.DMA((PARTS,)),
            pltpu.SemaphoreType.DMA((PARTS + 1,)),
        ],
        cost_estimate=pl.CostEstimate(flops=4 * n * width, bytes_accessed=4 * n * width, transcendentals=n),
        name="pack",
    )(valid_counts, embeddings, doc_ids)

    r1 = permute(own, plan.first)
    odd = permute(own, plan.swap_odd)
    moved = permute(own, plan.across)
    (own_0,) = stage(self_kernel, plan, at, [own], [], n, 1, 1, 1, 0, 1)
    own_a, moved_b = own[:half], moved[half:]
    r2 = permute(r1, plan.second)
    side = permute(odd, plan.side)
    top = permute(moved, plan.top)
    own_late, _ = lax.optimization_barrier((own, r1))
    even = permute(own_late, plan.swap_even)
    own_1, y_1, r1_1 = stage(first_kernel, plan, at, [own, r1, odd], [], n, 3, 2, 2, 1, 3)
    kin = permute(r2, plan.kin)
    own_a, moved_b, _ = lax.optimization_barrier((own_a, moved_b, r2))
    ua = permute(own_a, plan.gate_a)
    ub = permute(moved_b, plan.gate_b)
    own_2, y_2, r1_2, r2_2 = stage(second_kernel, plan, at, [own, r2, even, r1, odd], [y_1, r1_1], n, 4, 2, 2, 2, 4, held=[own, r2, even, r1])
    own_3, y_3, r1_3, side_3, kin_3 = stage(kin_kernel, plan, at, [own, kin, r1, side, odd], [y_2, r1_2], n, 5, 1, 4, 1, 4)
    own_4, y_4, top_4, side_4, u_4 = stage(gate_kernel, plan, at, [own, ua, ub, top, side, even, odd], [], n, 5, 1, 1, 4, 4, held=[own, ua, ub, top, side, even])

    returned = [
        permute(r2_2, plan.second_back),
        permute(r1_3, plan.first_back),
        permute(y_3, plan.swap),
        permute(side_3, plan.side_back),
        permute(kin_3, plan.kin_back),
        permute(u_4, plan.gate_back),
        permute(top_4, plan.top_back),
        permute(side_4, plan.side_back_late),
        permute(y_4, plan.swap_late),
    ]
    nearest = pl.pallas_call(
        functools.partial(finish_kernel, plan),
        out_shape=jax.ShapeDtypeStruct((n,), jnp.float32),
        in_specs=[SMEM, SMEM] + [VMEM] * 14,
        out_specs=VMEM,
        compiler_params=pltpu.CompilerParams(vmem_limit_bytes=SPARE),
        name="finish",
    )(at, valid_counts, own_0, own_1, own_2, own_3, own_4, *returned)
    return nearest


def solution(mesh):
    plan = Plan(mesh.shape["row"], mesh.shape["col"])

    def whole(embeddings, doc_ids, valid_counts):
        step = jax.shard_map(
            functools.partial(local, plan, doc_ids.shape[0]),
            mesh=mesh,
            in_specs=(P(AXES, None), P(AXES), P(AXES)),
            out_specs=P(AXES),
            check_vma=False,
        )
        return step(embeddings, doc_ids, valid_counts)

    return whole
```

```python
import functools
import math

import jax
import jax.numpy as jnp
from jax import lax
from jax.experimental import pallas as pl
from jax.experimental.pallas import tpu as pltpu
from jax.sharding import PartitionSpec as P


BAND = 4
Y = BAND // 2
HEAD = 16
TILE = 384
LANES = 128
PARTS = 6
SPARE = 4 << 20
AXES = ("row", "col")


class Plan:
    def __init__(self, rows, cols):
        self.R, self.Z, self.C = rows, cols // Y, cols
        Z, R = self.Z, self.R
        even, odd, gate = range(0, R, 2), range(1, R, 2), range(1, R - 1, 2)
        at, ys = self.at, range(Y)
        self.swap_odd = [(at(r, z, y), at(r, z, 1 - y)) for r in odd for z in range(Z) for y in ys]
        self.swap_even = [(at(r, z, y), at(r, z, 1 - y)) for r in even for z in range(Z) for y in ys]
        self.first = [(at(r, z, y), at(r, z - 1, y)) for r in even for z in range(1, Z) for y in ys]
        self.first += [(at(r, z, y), at(r, z + 1, y)) for r in odd for z in range(Z - 1) for y in ys]
        self.second = [(at(r, z, y), at(r, z - 1, y)) for r in even for z in range(1, Z - 1) for y in ys]
        self.second += [(at(r, z, y), at(r, z + 1, y)) for r in odd for z in range(1, Z - 1) for y in ys]
        self.side = [(at(r, 0, y), at(r, 1, y)) for r in odd for y in ys]
        self.side += [(at(r, Z - 1, y), at(r, Z - 2, y)) for r in gate for y in ys]
        self.kin = [(at(r, Z - 4, y), at(r + 1, 0, y)) for r in even for y in ys]
        self.kin += [(at(r, Z - 3, y), at(r + 1, 1, y)) for r in even for y in ys]
        self.across = [(at(r, Z - 1, y), at(r + 1, Z - 1, y)) for r in gate for y in ys]
        self.across += [(at(r + 1, 0, y), at(r, 0, y)) for r in gate for y in ys]
        self.top = [(at(r + 1, Z - 1, y), at(r, Z - 2, y)) for r in gate for y in ys]
        self.gate_a = [(at(r + 1, 0, y), at(r, Z - 2, y)) for r in gate for y in ys]
        self.gate_a += [(at(r, Z - 1, y), at(r + 1, 1, y)) for r in gate for y in ys]
        self.gate_b = [(at(r, 0, y), at(r, Z - 2, y)) for r in gate for y in ys]
        self.gate_b += [(at(r + 1, Z - 1, y), at(r + 1, 1, y)) for r in gate for y in ys]
        self.first_back = [(b, a) for a, b in self.first]
        self.second_back = [(at(r, z, y), at(r, z + 2, y)) for r in even for z in range(Z - 2) for y in ys]
        self.second_back += [(at(r, z, y), at(r, z - 2, y)) for r in odd for z in range(2, Z) for y in ys]
        self.side_back = [(at(r, 1, y), at(r, 0, 1 - y)) for r in odd for y in ys]
        self.side_back += [(at(r, Z - 2, y), at(r, Z - 1, 1 - y)) for r in gate for y in ys]
        self.top_back = [(at(r, 1, y), at(r, 0, y)) for r in odd for y in ys]
        self.top_back += [(at(r, Z - 2, y), at(r, Z - 1, y)) for r in gate for y in ys]
        self.row_back = [(at(r + 1, 0, y), at(r, Z - 2, y)) for r in even for y in ys]
        self.row_back += [(at(r + 1, 1, y), at(r, Z - 1, y)) for r in even for y in ys]
        self.row_back += [(b, a) for a, b in self.gate_a]
        self.swap = self.swap_even + self.swap_odd

    def at(self, r, z, y):
        return r * self.C + z * Y + y

    def place(self, index):
        r, c = index // self.C, index % self.C
        return r, c // Y, c % Y


def permute(block, pairs):
    return lax.ppermute(block, AXES, pairs)


def pack_kernel(docs, count_ref, emb_hbm, ids_ref, out_hbm, emb, out, in_sems, out_sems):
    n, width = emb_hbm.shape
    steps = in_sems.shape[0]
    size = n // steps

    def taken(i):
        rows = pl.ds(i * size, size)
        return pltpu.make_async_copy(emb_hbm.at[rows], emb.at[rows], in_sems.at[i])

    def given(i):
        rows = pl.ds(HEAD + i * size, size) if i < steps else pl.ds(0, HEAD)
        return pltpu.make_async_copy(out.at[rows], out_hbm.at[rows], out_sems.at[i])

    for i in range(steps):
        taken(i).start()
    lane = lax.broadcasted_iota(jnp.int32, (1, n), 1)
    code = jnp.where(lane < count_ref[0], docs - ids_ref[...].reshape(1, n), 0)
    row = lax.broadcasted_iota(jnp.int32, (HEAD, n), 0)
    head = jnp.where(row == 0, code & 255, jnp.where(row == 1, (code >> 8) & 255, jnp.where(row == 2, code >> 16, 0)))
    out[:HEAD, :n] = head.astype(jnp.float32).astype(jnp.bfloat16)
    if width > n:
        out[:HEAD, n:] = jnp.zeros((HEAD, width - n), jnp.bfloat16)
    given(steps).start()
    part = 32
    for i in range(steps):
        taken(i).wait()

        def scale(j, _):
            at = i * size + j * part
            x = emb[pl.ds(pl.multiple_of(at, HEAD), part), :].astype(jnp.float32)
            total = jnp.sum(x * x, axis=-1, keepdims=True)
            out[pl.ds(pl.multiple_of(HEAD + at, HEAD), part), :] = (x * lax.rsqrt(total + 1e-06)).astype(jnp.bfloat16)
            return 0

        lax.fori_loop(0, size // part, scale, 0, unroll=True)
        given(i).start()
    for i in range(steps + 1):
        given(i).wait()


def codes(ref, n):
    head = ref[:HEAD, :n].astype(jnp.float32)
    return head[0:1] + 256.0 * head[1:2] + 65536.0 * head[2:3]


def spread(row, out_ref):
    for g in range(row.shape[1] // LANES):
        block = jnp.broadcast_to(row[:, g * LANES : (g + 1) * LANES], (LANES, LANES))
        out_ref[g * LANES : (g + 1) * LANES, :] = block.T


def gather_rows(acc_ref):
    parts = [
        jnp.max(acc_ref[g * LANES : (g + 1) * LANES, :].T, axis=0, keepdims=True)
        for g in range(acc_ref.shape[0] // LANES)
    ]
    return jnp.concatenate(parts, axis=1)


def pair_job(left_ref, left_from, spread_ref, right_ref, right_codes, row_acc, col_acc, scores_ref, rows=None):
    start, stop = rows or (0, spread_ref.shape[0])
    n = right_codes.shape[1]
    groups = range(0, n, LANES)
    tiles = range((stop - start) // TILE)

    def multiply(i):
        scores_ref[i % 2] = lax.dot_general(
            left_ref[left_from + i * TILE : left_from + (i + 1) * TILE, :],
            right_ref[HEAD : HEAD + n, :],
            (((1,), (1,)), ((), ())),
            preferred_element_type=jnp.float32,
        )

    def reduce(i):
        ups = [None] * len(groups)
        theirs = [jnp.broadcast_to(right_codes[:, g : g + LANES], (8, LANES)) for g in groups]
        for j in range(0, TILE, 8):
            at = start + i * TILE + j
            mine = spread_ref[at : at + 8, :]
            best = row_acc[at : at + 8, :]
            for k, g in enumerate(groups):
                part = scores_ref[i % 2, j : j + 8, g : g + LANES]
                lower = theirs[k] > mine
                best = jnp.maximum(best, jnp.where(lower, part, -1.0))
                if col_acc is not None:
                    up = jnp.where(lower, -1.0, part)
                    ups[k] = up if ups[k] is None else jnp.maximum(ups[k], up)
            row_acc[at : at + 8, :] = best
        if col_acc is not None:
            for k, g in enumerate(groups):
                col_acc[:, g : g + LANES] = jnp.maximum(col_acc[:, g : g + LANES], ups[k])

    for i in tiles:
        multiply(i)
        if i > 0:
            reduce(i - 1)
    reduce(tiles[-1])


def clear(*refs):
    for ref in refs:
        ref[...] = jnp.full(ref.shape, -1.0, jnp.float32)


def put_rows(out_ref, acc_ref, *so_far):
    found = gather_rows(acc_ref)
    for ref in so_far:
        found = jnp.maximum(found, ref[...])
    out_ref[...] = found


def put_cols(out_ref, acc_ref, *so_far):
    found = jnp.max(acc_ref[...], axis=0, keepdims=True)
    for ref in so_far:
        found = jnp.maximum(found, ref[...])
    out_ref[...] = found


class Fetch:
    def __init__(self, needed, source, target, sem):
        self.needed, self.target = needed, target
        self.copy = pltpu.make_async_copy(source, target, sem)

    def start(self):
        if self.needed is True:
            self.copy.start()
        else:
            pl.when(self.needed)(self.copy.start)

    def wait(self):
        if self.needed is True:
            self.copy.wait()
        else:
            pl.when(self.needed)(self.copy.wait)
        return self.target


def fetches(refs, held, sems, needed):
    out = [Fetch(c, ref, h, sems.at[i]) for i, (ref, h, c) in enumerate(zip(refs, held, needed))]
    for f in out:
        f.start()
    return out


def position(plan, index_ref):
    index = index_ref[0]
    r, c = index // plan.C, index % plan.C
    return r, c // Y, c % Y, r % 2 == 0


def self_kernel(plan, index_ref, own_hbm, own_out, own_v, sems, scores, own_codes, own_best):
    n = own_codes.shape[0]
    (own,) = fetches([own_hbm], [own_v], sems, [True])
    clear(own_best)
    own = own.wait()
    row = codes(own, n)
    spread(row, own_codes)
    pair_job(own, HEAD, own_codes, own, row, own_best, None, scores)
    put_rows(own_out, own_best)


def first_kernel(plan, index_ref, own_hbm, r1_hbm, own_out, r1_out, own_v, r1_v, sems, scores, own_codes, own_best, r1_best):
    n = own_codes.shape[0]
    _, z, _, even = position(plan, index_ref)
    has_r1 = jnp.where(even, z <= plan.Z - 2, z >= 1)
    own, r1 = fetches([own_hbm, r1_hbm], [own_v, r1_v], sems, [has_r1, has_r1])
    clear(own_best, r1_best)
    own, r1 = own.wait(), r1.wait()

    @pl.when(has_r1)
    def _():
        spread(codes(own, n), own_codes)
        pair_job(own, HEAD, own_codes, r1, codes(r1, n), own_best, r1_best, scores)

    put_rows(own_out, own_best)
    put_cols(r1_out, r1_best)


def cross_kernel(plan, index_ref, own_hbm, odd_hbm, r1_hbm, r1_in, own_out, y_out, r1_out, own_v, odd_v, r1_v, sems, scores, y_codes, y_best, own_best, r1_best):
    n = y_codes.shape[0]
    _, z, _, even = position(plan, index_ref)
    odd = ~even
    has_r1 = odd & (z >= 1)
    own, other, r1 = fetches([own_hbm, odd_hbm, r1_hbm], [own_v, odd_v, r1_v], sems, [odd, odd, has_r1])
    clear(y_best, own_best, r1_best)
    own, other = own.wait(), other.wait()

    @pl.when(odd)
    def _():
        spread(codes(other, n), y_codes)
        pair_job(other, HEAD, y_codes, own, codes(own, n), y_best, own_best, scores)

    r1 = r1.wait()

    @pl.when(has_r1)
    def _():
        pair_job(other, HEAD, y_codes, r1, codes(r1, n), y_best, r1_best, scores)

    put_cols(own_out, own_best)
    put_rows(y_out, y_best)
    put_cols(r1_out, r1_best, r1_in)


def second_kernel(plan, index_ref, own_hbm, r2_hbm, even_hbm, r1_hbm, odd_hbm, y_in, r1_in, own_out, y_out, r1_out, r2_out, own_v, r2_v, y_v, r1_v, sems, scores, own_codes, y_codes, own_best, y_best, r1_best, r2_best):
    n = own_codes.shape[0]
    _, z, y, even = position(plan, index_ref)
    has_r1 = even & (z <= plan.Z - 2)
    has_r2 = jnp.where(even, z <= plan.Z - 3, z >= 2)
    late_y = (~even) & has_r2 & (y == 1)
    own, r2, lower, r1, upper = fetches(
        [own_hbm, r2_hbm, even_hbm, r1_hbm, odd_hbm], [own_v, r2_v, y_v, r1_v, y_v], sems, [True, has_r2, even, has_r1, late_y]
    )
    clear(own_best, y_best, r1_best, r2_best)
    own = own.wait()
    spread(codes(own, n), own_codes)
    r2 = r2.wait()

    @pl.when(has_r2)
    def _():
        pair_job(own, HEAD, own_codes, r2, codes(r2, n), own_best, r2_best, scores)

    held = lower.wait()
    upper.wait()

    @pl.when(even)
    def _():
        pair_job(own, HEAD, own_codes, held, codes(held, n), own_best, None, scores)

    @pl.when(even | late_y)
    def _():
        spread(codes(held, n), y_codes)

    @pl.when((even & has_r2 & (y == 0)) | late_y)
    def _():
        pair_job(held, HEAD, y_codes, r2, codes(r2, n), y_best, r2_best, scores)

    r1 = r1.wait()

    @pl.when(has_r1)
    def _():
        pair_job(held, HEAD, y_codes, r1, codes(r1, n), y_best, r1_best, scores)

    put_rows(own_out, own_best)
    put_rows(y_out, y_best, y_in)
    put_cols(r1_out, r1_best, r1_in)
    put_cols(r2_out, r2_best)


def kin_kernel(plan, index_ref, own_hbm, kin_hbm, r1_hbm, side_hbm, odd_hbm, y_in, own_out, y_out, r1_out, side_out, kin_out, own_v, kin_v, r1_v, side_v, odd_v, sems, scores, left_codes, own_best, y_best, r1_best, side_best, kin_best):
    n = left_codes.shape[0]
    _, z, y, even = position(plan, index_ref)
    here = (~even) & (z <= 1)
    both = (~even) & (z == 1)
    cross = here & (y == 1)
    own, kin, r1, side, odd = fetches(
        [own_hbm, kin_hbm, r1_hbm, side_hbm, odd_hbm], [own_v, kin_v, r1_v, side_v, odd_v], sems, [here, here, both, both, cross]
    )
    clear(own_best, y_best, r1_best, side_best, kin_best)
    own, kin = own.wait(), kin.wait()

    def meet(left, best):
        spread(codes(left, n), left_codes)
        pair_job(left, HEAD, left_codes, kin, codes(kin, n), best, kin_best, scores)

    @pl.when(here)
    def _():
        meet(own, own_best)

    r1, side = r1.wait(), side.wait()

    @pl.when(both)
    def _():
        meet(r1, r1_best)
        meet(side, side_best)

    odd = odd.wait()

    @pl.when(cross)
    def _():
        meet(odd, y_best)

    put_rows(own_out, own_best)
    put_rows(y_out, y_best, y_in)
    put_rows(r1_out, r1_best)
    put_rows(side_out, side_best)
    put_cols(kin_out, kin_best)


def gate_kernel(plan, index_ref, own_hbm, ua_hbm, ub_hbm, top_hbm, side_hbm, even_hbm, odd_hbm, y_in, top_in, side_in, u_in, own_out, y_out, top_out, side_out, u_out, own_v, ua_v, ub_v, top_v, side_v, y_v, sems, scores, u_codes, u_best, own_best, y_best, top_best, side_best):
    n = u_codes.shape[0]
    half = n // 2
    r, z, y, even = position(plan, index_ref)
    low = (~even) & (z == plan.Z - 2) & (r < plan.R - 1)
    high = even & (z == 1) & (r >= 2)
    here = low | high
    own, ua, ub, top, side, lower, upper = fetches(
        [own_hbm, ua_hbm, ub_hbm, top_hbm, side_hbm, even_hbm, odd_hbm],
        [own_v, ua_v, ub_v, top_v, side_v, y_v, y_v],
        sems,
        [here, here, here, low, low, high & (y == 1), low & (y == 0)],
    )
    clear(own_best, y_best, top_best, side_best, u_best)
    own, ua, ub = own.wait(), ua.wait(), ub.wait()

    def meet(right, best):
        row = codes(right, n)
        pair_job(ua, HEAD, u_codes, right, row, u_best, best, scores, (0, half))
        pair_job(ub, 0, u_codes, right, row, u_best, best, scores, (half, n))

    @pl.when(here)
    def _():
        spread(codes(ua, n), u_codes)
        meet(own, own_best)

    top, side = top.wait(), side.wait()

    @pl.when(low)
    def _():
        meet(top, top_best)
        meet(side, side_best)

    held = lower.wait()
    upper.wait()

    @pl.when((high & (y == 1)) | (low & (y == 0)))
    def _():
        meet(held, y_best)

    put_cols(own_out, own_best)
    put_cols(y_out, y_best, y_in)
    put_cols(top_out, top_best, top_in)
    put_cols(side_out, side_best, side_in)
    put_rows(u_out, u_best, u_in)


def finish_kernel(plan, index_ref, count_ref, own_0, own_1, own_2, own_3, own_4, own_5, second, first, row, top, side, swap, out_ref):
    r, z, _, even = position(plan, index_ref)
    Z, R = plan.Z, plan.R
    found = functools.reduce(jnp.maximum, [ref[...] for ref in (own_0, own_1, own_2, own_3, own_4, own_5, swap)])
    inner = (~even) & (r < R - 1)
    returns = (
        (second, jnp.where(even, z >= 2, z <= Z - 3)),
        (first, jnp.where(even, z >= 1, z <= Z - 2)),
        (row, jnp.where(even, (z >= Z - 2) | ((r >= 2) & (z == 0)), inner & (z == Z - 1))),
        (top, (~even) & ((z == 0) | (inner & (z == Z - 1)))),
        (side, (~even) & ((z == 0) | (inner & (z == Z - 1)))),
    )
    for ref, mine in returns:
        found = jnp.maximum(found, jnp.where(mine, ref[...], -1.0))
    lane = lax.broadcasted_iota(jnp.int32, found.shape, 1)
    out_ref[...] = jnp.where(lane < count_ref[0], found, -1.0).reshape(out_ref.shape)


SMEM, VMEM, ANY = (pl.BlockSpec(memory_space=m) for m in (pltpu.SMEM, pltpu.VMEM, pl.ANY))


def stage(kernel, plan, index, blocks, vectors, n, outs, spreads, rows, cols, jobs, held=None):
    vector = jax.ShapeDtypeStruct((1, n), jnp.float32)
    width = blocks[0].shape[1]
    held = blocks if held is None else held
    scratch = [pltpu.VMEM(b.shape, b.dtype) for b in held] + [pltpu.SemaphoreType.DMA((len(blocks),)), pltpu.VMEM((2, TILE, n), jnp.float32)]
    scratch += [pltpu.VMEM((n, LANES), jnp.float32)] * (spreads + rows) + [pltpu.VMEM((8, n), jnp.float32)] * cols
    used = sum(math.prod(b.shape) * 2 for b in held) + 4 * n * (2 * TILE + LANES * (spreads + rows) + 8 * cols)
    return pl.pallas_call(
        functools.partial(kernel, plan),
        compiler_params=pltpu.CompilerParams(vmem_limit_bytes=used + SPARE),
        out_shape=[vector] * outs,
        in_specs=[SMEM] + [ANY] * len(blocks) + [VMEM] * len(vectors),
        out_specs=[VMEM] * outs,
        scratch_shapes=scratch,
        cost_estimate=pl.CostEstimate(flops=2 * n * n * width * jobs, bytes_accessed=2 * n * width * len(blocks), transcendentals=0),
    )(index, *blocks, *vectors)


def local(plan, docs, embeddings, doc_ids, valid_counts):
    return body(plan, docs, embeddings, doc_ids, valid_counts)


def body(plan, docs, embeddings, doc_ids, valid_counts):
    n, width = embeddings.shape
    half = HEAD + n // 2
    at = (lax.axis_index("row") * plan.C + lax.axis_index("col")).astype(jnp.int32).reshape(1)
    own = pl.pallas_call(
        functools.partial(pack_kernel, docs),
        out_shape=jax.ShapeDtypeStruct((HEAD + n, width), jnp.bfloat16),
        in_specs=[SMEM, ANY, VMEM],
        out_specs=ANY,
        scratch_shapes=[
            pltpu.VMEM((n, width), jnp.bfloat16),
            pltpu.VMEM((HEAD + n, width), jnp.bfloat16),
            pltpu.SemaphoreType.DMA((PARTS,)),
            pltpu.SemaphoreType.DMA((PARTS + 1,)),
        ],
        cost_estimate=pl.CostEstimate(flops=4 * n * width, bytes_accessed=4 * n * width, transcendentals=n),
        name="pack",
    )(valid_counts, embeddings, doc_ids)

    r1 = permute(own, plan.first)
    odd = permute(own, plan.swap_odd)
    moved = permute(own, plan.across)
    (own_0,) = stage(self_kernel, plan, at, [own], [], n, 1, 1, 1, 0, 1)
    own_a = own[:half]
    moved_b = moved[half:]
    r2 = permute(r1, plan.second)
    side = permute(odd, plan.side)
    top = permute(moved, plan.top)
    own_late, _ = lax.optimization_barrier((own, r1))
    even = permute(own_late, plan.swap_even)
    own_1, r1_0 = stage(first_kernel, plan, at, [own, r1], [], n, 2, 1, 1, 1, 1)
    own_5, y_1, r1_1 = stage(cross_kernel, plan, at, [own, odd, r1], [r1_0], n, 3, 1, 1, 2, 2)
    kin = permute(r2, plan.kin)
    own_a, moved_b, _ = lax.optimization_barrier((own_a, moved_b, r2))
    ua = permute(own_a, plan.gate_a)
    ub = permute(moved_b, plan.gate_b)
    own_2, y_2, r1_2, r2_2 = stage(second_kernel, plan, at, [own, r2, even, r1, odd], [y_1, r1_1], n, 4, 2, 2, 2, 4, held=[own, r2, even, r1])
    own_3, y_3, r1_3, side_3, kin_3 = stage(kin_kernel, plan, at, [own, kin, r1, side, odd], [y_2], n, 5, 1, 4, 1, 4)
    own_4, y_4, top_4, side_4, u_4 = stage(gate_kernel, plan, at, [own, ua, ub, top, side, even, odd], [y_3, r1_3, side_3, kin_3], n, 5, 1, 1, 4, 4, held=[own, ua, ub, top, side, even])

    returned = [
        permute(r2_2, plan.second_back),
        permute(r1_2, plan.first_back),
        permute(u_4, plan.row_back),
        permute(top_4, plan.top_back),
        permute(side_4, plan.side_back),
        permute(y_4, plan.swap),
    ]
    nearest = pl.pallas_call(
        functools.partial(finish_kernel, plan),
        out_shape=jax.ShapeDtypeStruct((n,), jnp.float32),
        in_specs=[SMEM, SMEM] + [VMEM] * 12,
        out_specs=VMEM,
        compiler_params=pltpu.CompilerParams(vmem_limit_bytes=SPARE),
        name="finish",
    )(at, valid_counts, own_0, own_1, own_2, own_3, own_4, own_5, *returned)
    return nearest


def solution(mesh):
    plan = Plan(mesh.shape["row"], mesh.shape["col"])

    def whole(embeddings, doc_ids, valid_counts):
        step = jax.shard_map(
            functools.partial(local, plan, doc_ids.shape[0]),
            mesh=mesh,
            in_specs=(P(AXES, None), P(AXES), P(AXES)),
            out_specs=P(AXES),
            check_vma=False,
        )
        return step(embeddings, doc_ids, valid_counts)

    return whole
```
